32 devices in a mesh: frame: 8 (over z, x), row: 4 (over y, core).
Axes of the slice: x: 2, y: 2, z: 4, core: 2. Of those that a mesh axis runs over, the one named last changes fastest.
Arguments:
- frames: float32 [64, 128, 2048], P('frame', 'row'), may hold values from -12 to 12
Outputs:
- estimate: float32 [128, 2048], P('row')
The draws below stay inside these ranges and needn't reach their ends.
All inputs are finite; a program needn't handle non-finite values.
Results may differ from the reference program's by a relative error of at most 0.00002.
Values sent between devices are 32-bit elements; how exact they have to be, the bound alone decides.
No kernel may reach another device: no remote copies, remote signals or barrier semaphores. Data moves between devices by JAX's collectives and lax.ppermute only.
A program may use at most 64 MiB of HBM per device.

```python
import jax
import jax.numpy as jnp
from jax import lax

FRAMES = 64
ROUNDS = 3
COLS = 2048
HEIGHT = 128


def draw_frames(key, part):
    scene = jax.random.normal(jax.random.fold_in(key, 11), (HEIGHT, COLS), jnp.float32)
    shape = (FRAMES, HEIGHT, COLS)
    ladder = jnp.arange(FRAMES, dtype=jnp.float32) / (FRAMES - 1)
    jitter = jnp.exp(jax.random.uniform(jax.random.fold_in(key, 12), (FRAMES,), jnp.float32, -0.1, 0.1))
    gains = (0.5 + ladder) * jitter
    noise = 0.3 * jax.random.normal(jax.random.fold_in(key, 13), shape, jnp.float32)
    hits = jax.random.uniform(jax.random.fold_in(key, 14), shape, jnp.float32) < 0.06
    spikes = jax.random.uniform(jax.random.fold_in(key, 15), shape, jnp.float32, -4.0, 4.0)
    result = gains[:, None, None] * scene[None] + noise + jnp.where(hits, spikes, 0.0)
    return jnp.clip(result, -12.0, 12.0)


def setup_inputs(seed: int = 0) -> dict:
    key_list = jax.random.split(jax.random.key(seed), 2)
    return {
        "frames": draw_frames(jax.random.fold_in(key_list[1], 71), 0),
    }


GUIDE_EPS = 0.05
CAUCHY_SCALE = 0.5


def box_sum(field):
    height, width = field.shape
    padded = jnp.pad(field, ((4, 4), (4, 4)))
    rows_total = padded[0:height]
    for offset in range(1, 9):
        rows_total = rows_total + padded[offset:offset + height]
    total = rows_total[:, 0:width]
    for offset in range(1, 9):
        total = total + rows_total[:, offset:offset + width]
    return total


def reference(frames):
    counts = box_sum(jnp.ones(frames.shape[1:], jnp.float32))

    def smooth(field):
        return box_sum(field) / counts

    estimate = jnp.sum(frames, axis=0) / FRAMES
    for round_index in range(ROUNDS):
        mean_guide = smooth(estimate)
        variance = smooth(estimate * estimate) - mean_guide * mean_guide

        def accumulate(carry, frame):
            mean_frame = smooth(frame)
            cross = smooth(estimate * frame)
            slope = (cross - mean_guide * mean_frame) / (variance + GUIDE_EPS)
            offset_term = mean_frame - slope * mean_guide
            filtered = smooth(slope) * estimate + smooth(offset_term)
            gap = (filtered - estimate) / CAUCHY_SCALE
            weight = 1.0 / (1.0 + gap * gap)
            return (carry[0] + weight * frame, carry[1] + weight), None

        zeros = jnp.zeros_like(estimate)
        (weighted, total), unused = lax.scan(accumulate, (zeros, zeros), frames)
        estimate = weighted / total
    return estimate
```

```python
import functools

import jax
import jax.numpy as jnp
from jax import lax
from jax.experimental import pallas as pl
from jax.experimental.pallas import tpu as pltpu
from jax.sharding import PartitionSpec as P

ROUNDS = 3
RADIUS = 4
GUIDE_EPS = 0.05
CAUCHY_SCALE = 0.5

LANES = 128
GROUP = 8
BLOCK = 8
BOTH = ("frame", "row")


def lane_ids(shape):
    return lax.broadcasted_iota(jnp.int32, shape, len(shape) - 1)


def roll(x, shift):
    return pltpu.roll(x, shift % LANES, x.ndim - 1)


def col_box(v):
    s3 = v + roll(v, 1) + roll(v, -1)
    return s3 + roll(s3, 3) + roll(s3, -3)


def row_box(v):
    n = v.shape[0]
    s3 = v[0 : n - 2] + v[1 : n - 1] + v[2:n]
    return s3[0 : n - 8] + s3[3 : n - 5] + s3[6 : n - 2]


def count(place, limit):
    lower = jnp.maximum(place - RADIUS, 0)
    upper = jnp.minimum(place + RADIUS, limit - 1)
    return jnp.maximum(upper - lower + 1, 1).astype(jnp.float32)


def inverse_counts(first_row, rows, height, first_col, width):
    shape = (rows, GROUP, LANES)
    row = first_row + lax.broadcasted_iota(jnp.int32, shape, 0)
    col = first_col + lax.broadcasted_iota(jnp.int32, shape, 2)
    inside = jnp.logical_and(col >= 0, col < width)
    return jnp.where(inside, 1.0 / (count(row, height) * count(col, width)), 0.0)


def clear_edges(ref):
    zero = jnp.zeros((RADIUS, GROUP, LANES), jnp.float32)
    ref[0:RADIUS] = zero
    ref[ref.shape[0] - RADIUS :] = zero


def loop(total, step, body):
    def go(i, carry):
        body(pl.multiple_of(i * step, step))
        return carry

    lax.fori_loop(0, total // step, go, 0)


def pack_kernel(rows, x_ref, out_ref):
    half = rows // 2
    low = lane_ids((GROUP, LANES)) < LANES // 2
    for i in range(half):
        a = x_ref[pl.ds(i, GROUP, stride=rows), :]
        b = x_ref[pl.ds(i + half, GROUP, stride=rows), :]
        out_ref[0, i] = jnp.where(low, a, roll(b, 64))
        out_ref[1, i] = jnp.where(low, roll(a, 64), b)


def unpack_kernel(rows, r_ref, s_ref, left_ref, right_ref):
    n_row, half = r_ref.shape[0], rows // 2
    lane = lane_ids((GROUP, LANES))
    middle = jnp.logical_and(lane >= 32, lane < 96)
    slot = lane // 8

    def row_of(i):
        r, k = divmod(i, rows)
        v = r_ref[r, k % half]
        return v, k < half

    height = n_row * rows
    for p in range(height // 16):
        left = jnp.zeros((GROUP, LANES), jnp.float32)
        right = left
        for j in range(16):
            v, low = row_of(p * 16 + j)
            s_ref[p * 16 + j] = jnp.where(middle, roll(v, 32 if low else -32), 0.0)
            first = 0 if low else 64
            here = slot == j
            left = jnp.where(here, roll(v, 8 * j - first), left)
            right = jnp.where(here, roll(v, 8 * j - first - 56), right)
        left_ref[p] = left
        right_ref[p] = right


def stats_kernel(width, strip, s_ref, before_ref, after_ref, full_ref, mean_ref, est_ref, tmp, acc):
    g = pl.program_id(0)
    frames = pl.num_programs(0) * GROUP
    height = s_ref.shape[0]
    first_col = strip() * 64 - 32
    lane = lane_ids((GROUP, LANES))
    on_left = jnp.logical_and(lane >= 24, lane < 32)
    on_right = jnp.logical_and(lane >= 96, lane < 104)

    @pl.when(g == 0)
    def _():
        clear_edges(tmp)
        acc[...] = jnp.zeros_like(acc)

    def merge(i0):
        p = i0 // 16
        before, after = before_ref[p], after_ref[p]
        rows = []
        for j in range(16):
            v = s_ref[i0 + j]
            v = jnp.where(on_left, roll(before, 24 - 8 * j), v)
            v = jnp.where(on_right, roll(after, 96 - 8 * j), v)
            rows.append(v)
        v = jnp.stack(rows)
        full_ref[pl.ds(i0, 16)] = v
        acc[pl.ds(i0, 16)] += v
        tmp[pl.ds(i0 + RADIUS, 16)] = col_box(v)

    loop(height, 16, merge)

    def means(i0):
        ic = inverse_counts(i0, BLOCK, height, first_col, width)
        mean_ref[pl.ds(i0, BLOCK)] = row_box(tmp[pl.ds(i0, BLOCK + 8)]) * ic

    loop(height, BLOCK, means)

    @pl.when(g == pl.num_programs(0) - 1)
    def _():
        def finish(i0):
            est_ref[pl.ds(i0, BLOCK)] = jnp.sum(acc[pl.ds(i0, BLOCK)], axis=1) / frames

        loop(height, BLOCK, finish)


def round_kernel(
    width, strip, exchanged, last, n_frame, n_row,
    e_ref, before_ref, after_ref, s_ref, mean_ref, out_ref,
    est, guide, gain, mgain, scaled_e, scaled, twice, t1, t2, t3, acc_w, acc_t, flat,
):
    g = pl.program_id(0)
    height = s_ref.shape[0]
    first_col = strip() * 64 - 32

    @pl.when(g == 0)
    def _():
        clear_edges(t1)
        clear_edges(t2)
        clear_edges(t3)
        acc_w[...] = jnp.zeros_like(acc_w)
        acc_t[...] = jnp.zeros_like(acc_t)

        def spread(i0):
            e = e_ref[pl.ds(i0, BLOCK), :]
            if exchanged:
                lane = lane_ids(e.shape)
                e = jnp.where(lane < 32, roll(before_ref[pl.ds(i0, BLOCK), :], 64), e)
                e = jnp.where(lane >= 96, roll(after_ref[pl.ds(i0, BLOCK), :], 64), e)
            e = jnp.broadcast_to(e[:, None, :], (BLOCK, GROUP, LANES))
            est[pl.ds(i0, BLOCK)] = e
            t2[pl.ds(i0 + RADIUS, BLOCK)] = col_box(e)
            t3[pl.ds(i0 + RADIUS, BLOCK)] = col_box(e * e)

        loop(height, BLOCK, spread)

        def prepare(i0):
            here = pl.ds(i0, BLOCK)
            ic = inverse_counts(i0, BLOCK, height, first_col, width)
            m = row_box(t2[pl.ds(i0, BLOCK + 8)]) * ic
            var = row_box(t3[pl.ds(i0, BLOCK + 8)]) * ic - m * m
            inv = 1.0 / (var + GUIDE_EPS)
            e = est[here]
            guide[here] = m
            gain[here] = ic * inv
            mgain[here] = m * inv
            ic2 = ic * (1.0 / CAUCHY_SCALE)
            scaled[here] = ic2
            scaled_e[here] = ic2 * e
            twice[here] = e * (1.0 / CAUCHY_SCALE)

        loop(height, BLOCK, prepare)

    def product(i0):
        here = pl.ds(i0, BLOCK)
        t1[pl.ds(i0 + RADIUS, BLOCK)] = col_box(est[here] * s_ref[here])

    loop(height, BLOCK, product)

    def fit(i0):
        here = pl.ds(i0, BLOCK)
        cross = row_box(t1[pl.ds(i0, BLOCK + 8)])
        mean = mean_ref[here]
        slope = cross * gain[here] - mean * mgain[here]
        offset = mean - slope * guide[here]
        t2[pl.ds(i0 + RADIUS, BLOCK)] = col_box(slope)
        t3[pl.ds(i0 + RADIUS, BLOCK)] = col_box(offset)

    loop(height, BLOCK, fit)

    def weigh(i0):
        here = pl.ds(i0, BLOCK)
        a = row_box(t2[pl.ds(i0, BLOCK + 8)])
        b = row_box(t3[pl.ds(i0, BLOCK + 8)])
        gap = (a * scaled_e[here] + b * scaled[here]) - twice[here]
        weight = 1.0 / (1.0 + gap * gap)
        acc_w[here] += weight * s_ref[here]
        acc_t[here] += weight

    loop(height, BLOCK, weigh)

    @pl.when(g == pl.num_programs(0) - 1)
    def _():
        dest = flat if last else out_ref

        def finish(i0):
            here = pl.ds(i0, BLOCK)
            w = jnp.sum(acc_w[here], axis=1)
            t = jnp.sum(acc_t[here], axis=1)
            dest[here, :] = w / t

        loop(height, BLOCK, finish)
        if last:
            rows = height // n_row
            half = rows // 2
            low = lane_ids((half, LANES)) < 64
            for r in range(n_row):
                a = flat[rows * r : rows * r + half, :]
                b = flat[rows * r + half : rows * (r + 1), :]
                v = jnp.where(low, roll(a, -32), roll(b, 32))
                for f in range(n_frame):
                    out_ref[f, r] = v


def rows_kernel(r_ref, out_ref):
    half = r_ref.shape[1]
    low = lane_ids((half, LANES)) < 64
    for k in range(r_ref.shape[0] // 2):
        a, b = r_ref[2 * k], r_ref[2 * k + 1]
        here = slice(k * LANES, (k + 1) * LANES)
        out_ref[0:half, here] = jnp.where(low, a, roll(b, 64))
        out_ref[half : 2 * half, here] = jnp.where(low, roll(a, 64), b)


def strip_program(frames):
    n_frame, n_row = lax.axis_size("frame"), lax.axis_size("row")
    n_dev = n_frame * n_row
    local, rows, width = frames.shape
    height = rows * n_row
    half = rows // 2
    f32 = jnp.float32

    def strip():
        return lax.axis_index("frame") * n_row + lax.axis_index("row")

    packed = pl.pallas_call(
        functools.partial(pack_kernel, rows),
        grid=(width // LANES,),
        in_specs=[pl.BlockSpec((local * rows, LANES), lambda k: (0, k))],
        out_specs=pl.BlockSpec((2, half, GROUP, LANES), lambda k: (k, 0, 0, 0)),
        out_shape=jax.ShapeDtypeStruct((n_dev, half, GROUP, LANES), f32),
        name="pack",
    )(frames.reshape(local * rows, width))

    got = lax.all_to_all(packed, BOTH, 0, 0, tiled=True)

    tile = jax.ShapeDtypeStruct((height, n_frame * GROUP, LANES), f32)
    edge = jax.ShapeDtypeStruct((height // 16, n_frame * GROUP, LANES), f32)
    tile_spec = pl.BlockSpec((height, GROUP, LANES), lambda g: (0, g, 0))
    edge_spec = pl.BlockSpec((height // 16, GROUP, LANES), lambda g: (0, g, 0))
    field = pltpu.VMEM((height, GROUP, LANES), f32)
    padded = pltpu.VMEM((height + 2 * RADIUS, GROUP, LANES), f32)
    flat_spec = pl.BlockSpec((height, LANES), lambda g: (0, 0))
    flat = jax.ShapeDtypeStruct((height, LANES), f32)

    centre, left_edge, right_edge = pl.pallas_call(
        functools.partial(unpack_kernel, rows),
        grid=(n_frame,),
        in_specs=[pl.BlockSpec((n_row, half, GROUP, LANES), lambda g: (g, 0, 0, 0))],
        out_specs=(tile_spec, edge_spec, edge_spec),
        out_shape=(tile, edge, edge),
        name="unpack",
    )(got)

    up = [(i, i + 1) for i in range(n_dev - 1)]
    down = [(j, i) for i, j in up]

    def swap(to_left, to_right):
        return lax.ppermute(to_right, BOTH, up), lax.ppermute(to_left, BOTH, down)

    before, after = swap(left_edge, right_edge)
    full, mean, est = pl.pallas_call(
        functools.partial(stats_kernel, width, strip),
        grid=(n_frame,),
        in_specs=[tile_spec, edge_spec, edge_spec],
        out_specs=(tile_spec, tile_spec, flat_spec),
        out_shape=(tile, tile, flat),
        scratch_shapes=[padded, field],
        name="stats",
    )(centre, before, after)

    for k in range(ROUNDS):
        last = k == ROUNDS - 1
        before, after = swap(est, est) if k else (est, est)
        if last:
            out_shape = jax.ShapeDtypeStruct((n_frame, n_row, half, LANES), f32)
            out_spec = pl.BlockSpec(out_shape.shape, lambda g: (0, 0, 0, 0))
        else:
            out_shape, out_spec = flat, flat_spec
        est = pl.pallas_call(
            functools.partial(round_kernel, width, strip, k > 0, last, n_frame, n_row),
            grid=(n_frame,),
            in_specs=[flat_spec, flat_spec, flat_spec, tile_spec, tile_spec],
            out_specs=out_spec,
            out_shape=out_shape,
            scratch_shapes=[field] * 7 + [padded] * 3 + [field] * 2
            + [pltpu.VMEM((height, LANES), f32)],
            name="round",
        )(est, before, after, full, mean)

    got = lax.all_to_all(est.reshape(n_dev, half, LANES), BOTH, 0, 0, tiled=True)
    return pl.pallas_call(
        rows_kernel,
        out_shape=jax.ShapeDtypeStruct((rows, width), f32),
        name="rows",
    )(got)


def with_halo(x, dim, width):
    n, length = lax.axis_size("row"), x.shape[dim]
    up = [(i, i + 1) for i in range(n - 1)]
    down = [(j, i) for i, j in up]
    before = lax.ppermute(lax.slice_in_dim(x, length - width, length, axis=dim), "row", up)
    after = lax.ppermute(lax.slice_in_dim(x, 0, width, axis=dim), "row", down)
    return jnp.concatenate([before, x, after], axis=dim)


def smooth(padded_rows, area):
    length, width = padded_rows.shape[-2] - 8, padded_rows.shape[-1]
    total = sum(padded_rows[..., k : k + length, :] for k in range(9))
    padded = jnp.pad(total, [(0, 0)] * (total.ndim - 1) + [(4, 4)])
    return sum(padded[..., k : k + width] for k in range(9)) / area


def row_program(frames):
    rows, width = frames.shape[1:]
    height = rows * lax.axis_size("row")
    start = lax.axis_index("row") * rows
    total_frames = frames.shape[0] * lax.axis_size("frame")
    area = (
        count(start + jnp.arange(rows, dtype=jnp.int32), height)[:, None]
        * count(jnp.arange(width, dtype=jnp.int32), width)[None, :]
    )
    estimate = lax.psum(jnp.sum(frames, axis=0), "frame") / total_frames
    padded_frames = with_halo(frames, 1, 4)
    mean_frame = smooth(padded_frames, area)
    for _ in range(ROUNDS):
        padded = with_halo(estimate, 0, 4)
        guide = smooth(padded, area)
        variance = smooth(padded * padded, area) - guide * guide
        cross = smooth(padded[None] * padded_frames, area)
        slope = (cross - guide * mean_frame) / (variance + GUIDE_EPS)
        offset = mean_frame - slope * guide
        stacked = with_halo(jnp.stack((slope, offset)), 2, 4)
        filtered = smooth(stacked[0], area) * estimate[None] + smooth(stacked[1], area)
        gap = (filtered - estimate[None]) / CAUCHY_SCALE
        weight = 1.0 / (1.0 + gap * gap)
        sums = lax.psum((jnp.sum(weight * frames, axis=0), jnp.sum(weight, axis=0)), "frame")
        estimate = sums[0] / sums[1]
    return estimate


def shards(frames):
    local, rows, width = frames.shape
    n_dev = lax.axis_size("frame") * lax.axis_size("row")
    if local == GROUP and width == 64 * n_dev and rows % 16 == 0:
        return strip_program(frames)
    return row_program(frames)


def solution(mesh):
    return jax.shard_map(
        shards,
        mesh=mesh,
        in_specs=(P("frame", "row", None),),
        out_specs=P("row", None),
        check_vma=False,
    )
```

```python
import functools

import jax
import jax.numpy as jnp
from jax import lax
from jax.experimental import pallas as pl
from jax.experimental.pallas import tpu as pltpu
from jax.sharding import PartitionSpec as P

ROUNDS = 3
RADIUS = 4
GUIDE_EPS = 0.05
CAUCHY_SCALE = 0.5

LANES = 128
GROUP = 8
BOTH = ("frame", "row")


HALO = 2 * RADIUS
HALF = LANES // 2


def lane_ids(shape):
    return lax.broadcasted_iota(jnp.int32, shape, len(shape) - 1)


def roll(x, shift):
    return pltpu.roll(x, shift % LANES, x.ndim - 1)


def row_box(v):
    n = v.shape[0]
    s3 = v[0 : n - 2] + v[1 : n - 1] + v[2:n]
    return s3[0 : n - 8] + s3[3 : n - 5] + s3[6 : n - 2]


def col_box(ref, at, tmp):
    n = ref.shape[1] - HALO
    tmp[0 : n + 6] = ref[at, 0 : n + 6] + ref[at, 1 : n + 7] + ref[at, 2 : n + 8]
    return tmp[0:n] + tmp[3 : n + 3] + tmp[6 : n + 6]


def count(place, limit):
    lower = jnp.maximum(place - RADIUS, 0)
    upper = jnp.minimum(place + RADIUS, limit - 1)
    return jnp.maximum(upper - lower + 1, 1).astype(jnp.float32)


def loop(total, step, body):
    def go(i, carry):
        body(i * step)
        return carry

    lax.fori_loop(0, total // step, go, 0)


def halves_matrix():
    shape = (LANES, LANES)
    row = lax.broadcasted_iota(jnp.int32, shape, 0)
    return jnp.where((row < HALF) == (lane_ids(shape) < HALF), 1.0, 0.0).astype(jnp.bfloat16)


def frame_sum(x, ones):
    total = None
    for _ in range(3):
        part = x.astype(jnp.bfloat16)
        x = x - part.astype(jnp.float32)
        term = jnp.dot(part, ones, preferred_element_type=jnp.float32)
        total = term if total is None else total + term
    return total


def row_halo(ref, rows):
    width = ref.shape[1]
    lane = lane_ids((width, LANES))
    for k in range(HALO):
        ref[k] = jnp.where(lane >= HALF, roll(ref[rows + k], HALF), 0.0)
        ref[HALO + rows + k] = jnp.where(lane < HALF, roll(ref[HALO + k], HALF), 0.0)


def pack_kernel(rows, x_ref, out_ref, tmp):
    half = rows // 2
    low = lane_ids((GROUP, LANES)) < HALF
    for f in range(GROUP):
        tmp[f * (rows + 1) : f * (rows + 1) + rows] = x_ref[f * rows : (f + 1) * rows, :]
    for i in range(half):
        a = tmp[pl.ds(i, GROUP, stride=rows + 1), :]
        b = tmp[pl.ds(i + half, GROUP, stride=rows + 1), :]
        out_ref[0, i] = jnp.where(low, a, roll(b, HALF))
        out_ref[1, i] = jnp.where(low, roll(a, HALF), b)


def unpack_kernel(rows, r_ref, s_ref, left_ref, right_ref):
    groups, n_row, half = r_ref.shape[0:3]
    for r in range(n_row // 2):

        def go(i):
            parts = [r_ref[g, r + h * (n_row // 2), i] for h in range(2) for g in range(groups)]
            v = jnp.transpose(jnp.concatenate(parts, axis=0))
            for k in range(2):
                at = r * rows + k * half + i
                s_ref[at] = v[k * HALF : (k + 1) * HALF]
                left_ref[at] = v[k * HALF : k * HALF + HALO]
                right_ref[at] = v[(k + 1) * HALF - HALO : (k + 1) * HALF]

        loop(half, 1, go)


def stats_kernel(
    width, strip, s_ref, before_ref, after_ref, full_ref, mean_ref, area_ref, est_ref, boxed, tmp
):
    rows, cols = s_ref.shape[0:2]
    wide = cols + HALO
    height = 2 * rows
    first_col = strip() * cols - RADIUS
    ones = halves_matrix()

    def place(q):
        full_ref[q + HALO, 0:HALO] = before_ref[q]
        full_ref[q + HALO, HALO : HALO + cols] = s_ref[q]
        full_ref[q + HALO, HALO + cols :] = after_ref[q]

    loop(rows, 1, place)
    row_halo(full_ref, rows)

    def first(q):
        est_ref[q] = frame_sum(full_ref[q], ones) / HALF

    loop(rows + 2 * HALO, 1, first)

    step = rows // 8 * 3

    def down(q):
        for j in range(0, cols + 2 * HALO, 8):
            boxed[pl.ds(q, step), j : j + 8] = row_box(full_ref[pl.ds(q, step + HALO), j : j + 8])

    loop(rows + HALO, step, down)

    col = first_col + lax.broadcasted_iota(jnp.int32, (wide, LANES), 0)
    upper = jnp.where(lane_ids((wide, LANES)) < HALF, 0, rows)
    col_inverse = jnp.where(
        jnp.logical_and(col >= 0, col < width), 1.0 / count(col, width), 0.0
    )

    def means(q):
        row = q - RADIUS + upper
        inside = jnp.logical_and(row >= 0, row < height)
        area = jnp.where(inside, col_inverse / count(row, height), 0.0)
        area_ref[q] = area
        mean_ref[q] = col_box(boxed, q, tmp) * area

    loop(rows + HALO, 1, means)


def round_kernel(first, last, n_frame, n_row, *refs):
    e_ref, before_ref, after_ref, s_ref, mean_ref, area_ref = refs[0:6]
    outs, scratch = (refs[6:7], refs[7:]) if last else (refs[6:9], refs[9:])
    ext, b1, b2, b3, slope, offset, tmp, flat = scratch
    rows = mean_ref.shape[0] - HALO
    cols = mean_ref.shape[1] - HALO
    ones = halves_matrix()
    est = e_ref if first else ext
    edge_row = lane_ids((HALO, LANES)) % HALF

    if not first:
        def place(q):
            here = edge_row == q
            ext[q + HALO, 0:HALO] = frame_sum(jnp.where(here, before_ref[...], 0.0), ones)
            ext[q + HALO, HALO : HALO + cols] = e_ref[q]
            ext[q + HALO, HALO + cols :] = frame_sum(jnp.where(here, after_ref[...], 0.0), ones)

        loop(rows, 1, place)
        row_halo(ext, rows)

    step = rows // 8 * 3

    def down(q):
        for j in range(0, cols + 2 * HALO, 8):
            e = est[pl.ds(q, step + HALO), j : j + 8]
            b1[pl.ds(q, step), j : j + 8] = row_box(e * s_ref[pl.ds(q, step + HALO), j : j + 8])
            b2[pl.ds(q, step), j : j + 8] = row_box(e)
            b3[pl.ds(q, step), j : j + 8] = row_box(e * e)

    loop(rows + HALO, step, down)

    def fit(q0):
        for k in range(2):
            q = q0 + k
            area, mean = area_ref[q], mean_ref[q]
            guide = col_box(b2, q, tmp.at[3 * k]) * area
            variance = col_box(b3, q, tmp.at[3 * k + 1]) * area - guide * guide
            cross = col_box(b1, q, tmp.at[3 * k + 2]) * area
            a = (cross - guide * mean) / (variance + GUIDE_EPS)
            slope[q] = a
            offset[q] = mean - a * guide

    loop(rows + HALO, 2, fit)

    block = rows // 4

    def down_again(q):
        for j in range(0, cols + HALO, 8):
            b1[pl.ds(q, block), j : j + 8] = row_box(slope[pl.ds(q, block + HALO), j : j + 8])
            b2[pl.ds(q, block), j : j + 8] = row_box(offset[pl.ds(q, block + HALO), j : j + 8])

    loop(rows, block, down_again)

    lane = edge_row[0:1]

    def weigh(q0):
        for k in range(2):
            q = q0 + k
            area = area_ref[q + RADIUS, RADIUS : RADIUS + cols]
            e = est[q + HALO, HALO : HALO + cols]
            p = s_ref[q + HALO, HALO : HALO + cols]
            a = col_box(b1.at[:, 0 : cols + HALO], q, tmp.at[2 * k])
            b = col_box(b2.at[:, 0 : cols + HALO], q, tmp.at[2 * k + 1])
            gap = ((a * e + b) * area - e) * (1.0 / CAUCHY_SCALE)
            weight = 1.0 / (1.0 + gap * gap)
            new = frame_sum(weight * p, ones) / frame_sum(weight, ones)
            if last:
                flat[...] = jnp.where(lane == q, new, flat[...])
            else:
                outs[0][q] = new
                here = edge_row == q
                outs[1][...] = jnp.where(here, new[0:HALO], outs[1][...])
                outs[2][...] = jnp.where(here, new[cols - HALO :], outs[2][...])

    if last:
        flat[...] = jnp.zeros_like(flat)
    else:
        outs[1][...] = jnp.zeros_like(outs[1])
        outs[2][...] = jnp.zeros_like(outs[2])
    loop(rows, 2, weigh)

    if last:
        shard = 2 * rows // n_row
        half = shard // 2
        turned = jnp.transpose(jnp.concatenate([flat[...], roll(flat[...], -half)], axis=0))
        for r in range(n_row):
            for f in range(n_frame):
                outs[0][f, r] = turned[r * shard : r * shard + half]


def rows_kernel(r_ref, out_ref):
    half = r_ref.shape[1]
    low = lane_ids((half, LANES)) < HALF
    for k in range(r_ref.shape[0] // 2):
        a, b = r_ref[2 * k], r_ref[2 * k + 1]
        here = slice(k * LANES, (k + 1) * LANES)
        out_ref[0:half, here] = jnp.where(low, a, roll(b, HALF))
        out_ref[half : 2 * half, here] = jnp.where(low, roll(a, HALF), b)


def strip_program(frames):
    n_frame, n_row = lax.axis_size("frame"), lax.axis_size("row")
    n_dev = n_frame * n_row
    local, rows, width = frames.shape
    half = rows // 2
    deep = rows * n_row // 2
    cols = width // n_dev
    f32 = jnp.float32

    def array(*shape):
        return jax.ShapeDtypeStruct(shape + (LANES,), f32)

    def scratch(*shape):
        return pltpu.VMEM(shape + (LANES,), f32)

    def strip():
        return lax.axis_index("frame") * n_row + lax.axis_index("row")

    packed = pl.pallas_call(
        functools.partial(pack_kernel, rows),
        grid=(width // LANES,),
        in_specs=[pl.BlockSpec((local * rows, LANES), lambda k: (0, k))],
        out_specs=pl.BlockSpec((2, half, GROUP, LANES), lambda k: (k, 0, 0, 0)),
        out_shape=array(n_dev, half, GROUP),
        scratch_shapes=[scratch(GROUP * (rows + 1))],
        name="pack",
    )(frames.reshape(local * rows, width))

    got = lax.all_to_all(packed, BOTH, 0, 0, tiled=True)

    edge = array(deep, HALO)
    centre, left_edge, right_edge = pl.pallas_call(
        functools.partial(unpack_kernel, rows),
        out_shape=(array(deep, cols), edge, edge),
        name="unpack",
    )(got.reshape(n_frame, n_row, half, GROUP, LANES))

    up = [(i, i + 1) for i in range(n_dev - 1)]
    down = [(j, i) for i, j in up]

    def swap(to_left, to_right):
        return lax.ppermute(to_right, BOTH, up), lax.ppermute(to_left, BOTH, down)

    before, after = swap(left_edge, right_edge)
    whole = (deep + 2 * HALO, cols + 2 * HALO)
    fitted = (deep + HALO, cols + HALO)
    full, mean, area, est = pl.pallas_call(
        functools.partial(stats_kernel, width, strip),
        out_shape=(array(*whole), array(*fitted), array(*fitted), array(*whole)),
        scratch_shapes=[scratch(fitted[0], whole[1]), scratch(whole[1])],
        name="stats",
    )(centre, before, after)

    before = after = jnp.zeros((HALO, LANES), f32)
    for k in range(ROUNDS):
        first, last = k == 0, k == ROUNDS - 1
        if not first:
            before, after = swap(left_edge, right_edge)
        if last:
            out_shape = array(n_frame, n_row, half)
        else:
            out_shape = (array(deep, cols), array(HALO), array(HALO))
        result = pl.pallas_call(
            functools.partial(round_kernel, first, last, n_frame, n_row),
            out_shape=out_shape,
            scratch_shapes=[scratch(*whole)]
            + [scratch(fitted[0], whole[1])] * 3
            + [scratch(*fitted)] * 2
            + [scratch(6, whole[1]), scratch(cols)],
            name="round",
        )(est, before, after, full, mean, area)
        if not last:
            est, left_edge, right_edge = result

    got = lax.all_to_all(result.reshape(n_dev, half, LANES), BOTH, 0, 0, tiled=True)
    return pl.pallas_call(
        rows_kernel,
        out_shape=jax.ShapeDtypeStruct((rows, width), f32),
        name="rows",
    )(got)


def with_halo(x, dim, width):
    n, length = lax.axis_size("row"), x.shape[dim]
    up = [(i, i + 1) for i in range(n - 1)]
    down = [(j, i) for i, j in up]
    before = lax.ppermute(lax.slice_in_dim(x, length - width, length, axis=dim), "row", up)
    after = lax.ppermute(lax.slice_in_dim(x, 0, width, axis=dim), "row", down)
    return jnp.concatenate([before, x, after], axis=dim)


def smooth(padded_rows, area):
    length, width = padded_rows.shape[-2] - 8, padded_rows.shape[-1]
    total = sum(padded_rows[..., k : k + length, :] for k in range(9))
    padded = jnp.pad(total, [(0, 0)] * (total.ndim - 1) + [(4, 4)])
    return sum(padded[..., k : k + width] for k in range(9)) / area


def row_program(frames):
    rows, width = frames.shape[1:]
    height = rows * lax.axis_size("row")
    start = lax.axis_index("row") * rows
    total_frames = frames.shape[0] * lax.axis_size("frame")
    area = (
        count(start + jnp.arange(rows, dtype=jnp.int32), height)[:, None]
        * count(jnp.arange(width, dtype=jnp.int32), width)[None, :]
    )
    estimate = lax.psum(jnp.sum(frames, axis=0), "frame") / total_frames
    padded_frames = with_halo(frames, 1, 4)
    mean_frame = smooth(padded_frames, area)
    for _ in range(ROUNDS):
        padded = with_halo(estimate, 0, 4)
        guide = smooth(padded, area)
        variance = smooth(padded * padded, area) - guide * guide
        cross = smooth(padded[None] * padded_frames, area)
        slope = (cross - guide * mean_frame) / (variance + GUIDE_EPS)
        offset = mean_frame - slope * guide
        stacked = with_halo(jnp.stack((slope, offset)), 2, 4)
        filtered = smooth(stacked[0], area) * estimate[None] + smooth(stacked[1], area)
        gap = (filtered - estimate[None]) / CAUCHY_SCALE
        weight = 1.0 / (1.0 + gap * gap)
        sums = lax.psum((jnp.sum(weight * frames, axis=0), jnp.sum(weight, axis=0)), "frame")
        estimate = sums[0] / sums[1]
    return estimate


def shards(frames):
    local, rows, width = frames.shape
    n_dev = lax.axis_size("frame") * lax.axis_size("row")
    strips = local == GROUP and local * lax.axis_size("frame") == LANES // 2
    strips = strips and 2 * width == LANES * n_dev and rows % 16 == 0
    strips = strips and rows * lax.axis_size("row") % LANES == 0 and lax.axis_size("row") % 2 == 0
    if strips and rows * lax.axis_size("row") == LANES:
        return strip_program(frames)
    return row_program(frames)


def solution(mesh):
    return jax.shard_map(
        shards,
        mesh=mesh,
        in_specs=(P("frame", "row", None),),
        out_specs=P("row", None),
        check_vma=False,
    )
```

```python
import functools

import jax
import jax.numpy as jnp
from jax import lax
from jax.experimental import pallas as pl
from jax.experimental.pallas import tpu as pltpu
from jax.sharding import PartitionSpec as P

ROUNDS = 3
RADIUS = 4
GUIDE_EPS = 0.05
CAUCHY_SCALE = 0.5

LANES = 128
GROUP = 8
BOTH = ("frame", "row")


HALO = 2 * RADIUS
HALF = LANES // 2


def lane_ids(shape):
    return lax.broadcasted_iota(jnp.int32, shape, len(shape) - 1)


def roll(x, shift):
    return pltpu.roll(x, shift % LANES, x.ndim - 1)


def row_box(v):
    n = v.shape[0]
    s3 = v[0 : n - 2] + v[1 : n - 1] + v[2:n]
    return s3[0 : n - 8] + s3[3 : n - 5] + s3[6 : n - 2]


def col_box(ref, at, tmp):
    n = ref.shape[1] - HALO
    tmp[0 : n + 6] = ref[at, 0 : n + 6] + ref[at, 1 : n + 7] + ref[at, 2 : n + 8]
    return tmp[0:n] + tmp[3 : n + 3] + tmp[6 : n + 6]


def count(place, limit):
    lower = jnp.maximum(place - RADIUS, 0)
    upper = jnp.minimum(place + RADIUS, limit - 1)
    return jnp.maximum(upper - lower + 1, 1).astype(jnp.float32)


def loop(total, step, body):
    def go(i, carry):
        body(i * step)
        return carry

    lax.fori_loop(0, total // step, go, 0)


def halves_matrix():
    shape = (LANES, LANES)
    row = lax.broadcasted_iota(jnp.int32, shape, 0)
    return jnp.where((row < HALF) == (lane_ids(shape) < HALF), 1.0, 0.0).astype(jnp.bfloat16)


def frame_sum(x, ones):
    total = None
    for _ in range(3):
        part = x.astype(jnp.bfloat16)
        x = x - part.astype(jnp.float32)
        term = jnp.dot(part, ones, preferred_element_type=jnp.float32)
        total = term if total is None else total + term
    return total


def row_halo(ref, rows):
    width = ref.shape[1]
    lane = lane_ids((width, LANES))
    for k in range(HALO):
        ref[k] = jnp.where(lane >= HALF, roll(ref[rows + k], HALF), 0.0)
        ref[HALO + rows + k] = jnp.where(lane < HALF, roll(ref[HALO + k], HALF), 0.0)


def pack_kernel(rows, x_ref, out_ref, tmp):
    half = rows // 2
    low = lane_ids((GROUP, LANES)) < HALF
    for k in range(x_ref.shape[1] // LANES):
        here = slice(k * LANES, (k + 1) * LANES)
        for f in range(GROUP):
            tmp[k, f * (rows + 1) : f * (rows + 1) + rows] = x_ref[f * rows : (f + 1) * rows, here]
        for i in range(half):
            a = tmp[k, pl.ds(i, GROUP, stride=rows + 1), :]
            b = tmp[k, pl.ds(i + half, GROUP, stride=rows + 1), :]
            out_ref[2 * k, i] = jnp.where(low, a, roll(b, HALF))
            out_ref[2 * k + 1, i] = jnp.where(low, roll(a, HALF), b)


def unpack_kernel(rows, r_ref, s_ref, left_ref, right_ref):
    groups, n_row, half = r_ref.shape[0:3]
    for r in range(n_row // 2):

        def go(i):
            parts = [r_ref[g, r + h * (n_row // 2), i] for h in range(2) for g in range(groups)]
            v = jnp.transpose(jnp.concatenate(parts, axis=0))
            for k in range(2):
                at = r * rows + k * half + i
                s_ref[at] = v[k * HALF : (k + 1) * HALF]
                left_ref[at] = v[k * HALF : k * HALF + HALO]
                right_ref[at] = v[(k + 1) * HALF - HALO : (k + 1) * HALF]

        loop(half, 1, go)


def prepare(width, strip, s_ref, before_ref, after_ref, full_ref, mean_ref, area_ref, est, boxed, tmp):
    rows, cols = s_ref.shape[0:2]
    wide = cols + HALO
    height = 2 * rows
    first_col = strip() * cols - RADIUS
    ones = halves_matrix()

    def place(q0):
        for q in (q0, q0 + 1, q0 + 2, q0 + 3):
            full_ref[q + HALO, 0:HALO] = before_ref[q]
            full_ref[q + HALO, HALO : HALO + cols] = s_ref[q]
            full_ref[q + HALO, HALO + cols :] = after_ref[q]

    loop(rows, 4, place)
    row_halo(full_ref, rows)

    def first(q):
        v = full_ref[pl.ds(q, 4)]
        est[pl.ds(q, 4)] = (frame_sum(v.reshape(-1, LANES), ones) / HALF).reshape(v.shape)

    loop(rows + 2 * HALO, 4, first)

    step = rows // 8 * 3

    def down(q):
        for j in range(0, cols + 2 * HALO, 8):
            boxed[pl.ds(q, step), j : j + 8] = row_box(full_ref[pl.ds(q, step + HALO), j : j + 8])

    loop(rows + HALO, step, down)

    col = first_col + lax.broadcasted_iota(jnp.int32, (wide, LANES), 0)
    upper = jnp.where(lane_ids((8, LANES)) < HALF, 0, rows)
    col_inverse = jnp.where(
        jnp.logical_and(col >= 0, col < width), 1.0 / count(col, width), 0.0
    )

    def means(q0):
        for k in range(4):
            q = q0 + k
            row = q - RADIUS + upper
            inside = jnp.logical_and(row >= 0, row < height)
            row_inverse = jnp.where(inside, 1.0 / count(row, height), 0.0)
            area = col_inverse * jnp.concatenate([row_inverse] * (wide // 8), axis=0)
            area_ref[q] = area
            mean_ref[q] = col_box(boxed, q, tmp.at[k]) * area

    loop(rows + HALO, 4, means)


def round_kernel(first, last, width, strip, n_frame, n_row, *refs):
    if first:
        centre_ref, before_ref, after_ref = refs[0:3]
        outs, (s_ref, mean_ref, area_ref), scratch = refs[3:6], refs[6:9], refs[9:]
    else:
        e_ref, before_ref, after_ref, s_ref, mean_ref, area_ref = refs[0:6]
        outs, scratch = (refs[6:7], refs[7:]) if last else (refs[6:9], refs[9:])
    est, b1, b2, b3, slope, offset, tmp, w_buf, t_buf, flat = scratch
    rows = mean_ref.shape[0] - HALO
    cols = mean_ref.shape[1] - HALO
    ones = halves_matrix()
    edge_row = lane_ids((HALO, LANES)) % HALF

    if first:
        prepare(
            width, strip, centre_ref, before_ref, after_ref, s_ref, mean_ref, area_ref, est, b1, tmp
        )
    else:
        def place(q0):
            edges = [
                jnp.where(edge_row == q0 + k, ref[...], 0.0)
                for ref in (before_ref, after_ref)
                for k in range(8)
            ]
            v = frame_sum(jnp.concatenate(edges, axis=0), ones)
            for k in range(8):
                q = q0 + k
                est[q + HALO, 0:HALO] = v[HALO * k : HALO * (k + 1)]
                est[q + HALO, HALO : HALO + cols] = e_ref[q]
                est[q + HALO, HALO + cols :] = v[HALO * (8 + k) : HALO * (9 + k)]

        loop(rows, 8, place)
        row_halo(est, rows)

    step = rows // 8 * 3

    def down(q):
        for j in range(0, cols + 2 * HALO, 8):
            e = est[pl.ds(q, step + HALO), j : j + 8]
            b1[pl.ds(q, step), j : j + 8] = row_box(e * s_ref[pl.ds(q, step + HALO), j : j + 8])
            b2[pl.ds(q, step), j : j + 8] = row_box(e)
            b3[pl.ds(q, step), j : j + 8] = row_box(e * e)

    loop(rows + HALO, step, down)

    def fit(q0):
        for k in range(2):
            q = q0 + k
            area, mean = area_ref[q], mean_ref[q]
            guide = col_box(b2, q, tmp.at[3 * k]) * area
            variance = col_box(b3, q, tmp.at[3 * k + 1]) * area - guide * guide
            cross = col_box(b1, q, tmp.at[3 * k + 2]) * area
            a = (cross - guide * mean) / (variance + GUIDE_EPS)
            slope[q] = a
            offset[q] = mean - a * guide

    loop(rows + HALO, 2, fit)

    block = rows // 4

    def down_again(q):
        for j in range(0, cols + HALO, 8):
            b1[pl.ds(q, block), j : j + 8] = row_box(slope[pl.ds(q, block + HALO), j : j + 8])
            b2[pl.ds(q, block), j : j + 8] = row_box(offset[pl.ds(q, block + HALO), j : j + 8])

    loop(rows, block, down_again)

    lane = edge_row[0:1]

    def weigh(q0):
        for k in range(2):
            q = q0 + k
            area = area_ref[q + RADIUS, RADIUS : RADIUS + cols]
            e = est[q + HALO, HALO : HALO + cols]
            p = s_ref[q + HALO, HALO : HALO + cols]
            a = col_box(b1.at[:, 0 : cols + HALO], q, tmp.at[2 * k])
            b = col_box(b2.at[:, 0 : cols + HALO], q, tmp.at[2 * k + 1])
            gap = ((a * e + b) * area - e) * (1.0 / CAUCHY_SCALE)
            weight = 1.0 / (1.0 + gap * gap)
            w_buf[q] = weight * p
            t_buf[q] = weight

    loop(rows, 2, weigh)

    if last:
        flat[...] = jnp.zeros_like(flat)
    else:
        outs[1][...] = jnp.zeros_like(outs[1])
        outs[2][...] = jnp.zeros_like(outs[2])

    def merge(q0):
        w = frame_sum(w_buf[pl.ds(q0, 4)].reshape(4 * cols, LANES), ones)
        t = frame_sum(t_buf[pl.ds(q0, 4)].reshape(4 * cols, LANES), ones)
        new = (w / t).reshape(4, cols, LANES)
        if last:
            v = flat[...]
            for k in range(4):
                v = jnp.where(lane == q0 + k, new[k], v)
            flat[...] = v
        else:
            outs[0][pl.ds(q0, 4)] = new
            left, right = outs[1][...], outs[2][...]
            for k in range(4):
                here = edge_row == q0 + k
                left = jnp.where(here, new[k, 0:HALO], left)
                right = jnp.where(here, new[k, cols - HALO :], right)
            outs[1][...] = left
            outs[2][...] = right

    loop(rows, 4, merge)

    if last:
        shard = 2 * rows // n_row
        half = shard // 2
        turned = jnp.transpose(jnp.concatenate([flat[...], roll(flat[...], -half)], axis=0))
        for r in range(n_row):
            for f in range(n_frame):
                outs[0][f, r] = turned[r * shard : r * shard + half]


def rows_kernel(r_ref, out_ref):
    half = r_ref.shape[1]
    low = lane_ids((half, LANES)) < HALF
    for k in range(r_ref.shape[0] // 2):
        a, b = r_ref[2 * k], r_ref[2 * k + 1]
        here = slice(k * LANES, (k + 1) * LANES)
        out_ref[0:half, here] = jnp.where(low, a, roll(b, HALF))
        out_ref[half : 2 * half, here] = jnp.where(low, roll(a, HALF), b)


def strip_program(frames):
    n_frame, n_row = lax.axis_size("frame"), lax.axis_size("row")
    n_dev = n_frame * n_row
    local, rows, width = frames.shape
    half = rows // 2
    deep = rows * n_row // 2
    cols = width // n_dev
    f32 = jnp.float32

    def array(*shape):
        return jax.ShapeDtypeStruct(shape + (LANES,), f32)

    def scratch(*shape):
        return pltpu.VMEM(shape + (LANES,), f32)

    def strip():
        return lax.axis_index("frame") * n_row + lax.axis_index("row")

    packed = pl.pallas_call(
        functools.partial(pack_kernel, rows),
        grid=(4,),
        in_specs=[pl.BlockSpec((local * rows, width // 4), lambda k: (0, k))],
        out_specs=pl.BlockSpec((n_dev // 4, half, GROUP, LANES), lambda k: (k, 0, 0, 0)),
        out_shape=array(n_dev, half, GROUP),
        scratch_shapes=[scratch(width // 4 // LANES, GROUP * (rows + 1))],
        name="pack",
    )(frames.reshape(local * rows, width))

    got = lax.all_to_all(packed, BOTH, 0, 0, tiled=True)

    edge = array(deep, HALO)
    centre, left_edge, right_edge = pl.pallas_call(
        functools.partial(unpack_kernel, rows),
        out_shape=(array(deep, cols), edge, edge),
        name="unpack",
    )(got.reshape(n_frame, n_row, half, GROUP, LANES))

    up = [(i, i + 1) for i in range(n_dev - 1)]
    down = [(j, i) for i, j in up]

    def swap(to_left, to_right):
        return lax.ppermute(to_right, BOTH, up), lax.ppermute(to_left, BOTH, down)

    before, after = swap(left_edge, right_edge)
    whole = (deep + 2 * HALO, cols + 2 * HALO)
    fitted = (deep + HALO, cols + HALO)
    work = [scratch(*whole)] + [scratch(fitted[0], whole[1])] * 3 + [scratch(*fitted)] * 2
    work += [scratch(6, whole[1]), scratch(deep, cols), scratch(deep, cols), scratch(cols)]
    estimate_out = (array(deep, cols), array(HALO), array(HALO))

    def run_round(k, *operands):
        first, last = k == 0, k == ROUNDS - 1
        if last:
            out_shape = array(n_frame, n_row, half)
        elif first:
            out_shape = estimate_out + (array(*whole), array(*fitted), array(*fitted))
        else:
            out_shape = estimate_out
        return pl.pallas_call(
            functools.partial(round_kernel, first, last, width, strip, n_frame, n_row),
            out_shape=out_shape,
            scratch_shapes=work,
            name="round",
        )(*operands)

    est, left_edge, right_edge, *fixed = run_round(0, centre, before, after)
    for k in range(1, ROUNDS):
        before, after = swap(left_edge, right_edge)
        result = run_round(k, est, before, after, *fixed)
        if k < ROUNDS - 1:
            est, left_edge, right_edge = result

    got = lax.all_to_all(result.reshape(n_dev, half, LANES), BOTH, 0, 0, tiled=True)
    return pl.pallas_call(
        rows_kernel,
        out_shape=jax.ShapeDtypeStruct((rows, width), f32),
        name="rows",
    )(got)


def with_halo(x, dim, width):
    n, length = lax.axis_size("row"), x.shape[dim]
    up = [(i, i + 1) for i in range(n - 1)]
    down = [(j, i) for i, j in up]
    before = lax.ppermute(lax.slice_in_dim(x, length - width, length, axis=dim), "row", up)
    after = lax.ppermute(lax.slice_in_dim(x, 0, width, axis=dim), "row", down)
    return jnp.concatenate([before, x, after], axis=dim)


def smooth(padded_rows, area):
    length, width = padded_rows.shape[-2] - 8, padded_rows.shape[-1]
    total = sum(padded_rows[..., k : k + length, :] for k in range(9))
    padded = jnp.pad(total, [(0, 0)] * (total.ndim - 1) + [(4, 4)])
    return sum(padded[..., k : k + width] for k in range(9)) / area


def row_program(frames):
    rows, width = frames.shape[1:]
    height = rows * lax.axis_size("row")
    start = lax.axis_index("row") * rows
    total_frames = frames.shape[0] * lax.axis_size("frame")
    area = (
        count(start + jnp.arange(rows, dtype=jnp.int32), height)[:, None]
        * count(jnp.arange(width, dtype=jnp.int32), width)[None, :]
    )
    estimate = lax.psum(jnp.sum(frames, axis=0), "frame") / total_frames
    padded_frames = with_halo(frames, 1, 4)
    mean_frame = smooth(padded_frames, area)
    for _ in range(ROUNDS):
        padded = with_halo(estimate, 0, 4)
        guide = smooth(padded, area)
        variance = smooth(padded * padded, area) - guide * guide
        cross = smooth(padded[None] * padded_frames, area)
        slope = (cross - guide * mean_frame) / (variance + GUIDE_EPS)
        offset = mean_frame - slope * guide
        stacked = with_halo(jnp.stack((slope, offset)), 2, 4)
        filtered = smooth(stacked[0], area) * estimate[None] + smooth(stacked[1], area)
        gap = (filtered - estimate[None]) / CAUCHY_SCALE
        weight = 1.0 / (1.0 + gap * gap)
        sums = lax.psum((jnp.sum(weight * frames, axis=0), jnp.sum(weight, axis=0)), "frame")
        estimate = sums[0] / sums[1]
    return estimate


def shards(frames):
    local, rows, width = frames.shape
    n_dev = lax.axis_size("frame") * lax.axis_size("row")
    strips = local == GROUP and local * lax.axis_size("frame") == LANES // 2
    strips = strips and 2 * width == LANES * n_dev and rows % 16 == 0
    strips = strips and rows * lax.axis_size("row") % LANES == 0 and lax.axis_size("row") % 2 == 0
    if strips and rows * lax.axis_size("row") == LANES:
        return strip_program(frames)
    return row_program(frames)


def solution(mesh):
    return jax.shard_map(
        shards,
        mesh=mesh,
        in_specs=(P("frame", "row", None),),
        out_specs=P("row", None),
        check_vma=False,
    )
```

```python
import functools

import jax
import jax.numpy as jnp
from jax import lax
from jax.experimental import pallas as pl
from jax.experimental.pallas import tpu as pltpu
from jax.sharding import PartitionSpec as P

ROUNDS = 3
RADIUS = 4
GUIDE_EPS = 0.05
CAUCHY_SCALE = 0.5

LANES = 128
GROUP = 8
BOTH = ("frame", "row")


HALO = 2 * RADIUS
HALF = LANES // 2


def lane_ids(shape):
    return lax.broadcasted_iota(jnp.int32, shape, len(shape) - 1)


def roll(x, shift):
    return pltpu.roll(x, shift % LANES, x.ndim - 1)


def row_box(v):
    n = v.shape[0]
    s3 = v[0 : n - 2] + v[1 : n - 1] + v[2:n]
    return s3[0 : n - 8] + s3[3 : n - 5] + s3[6 : n - 2]


def col_box(ref, at, tmp):
    n = ref.shape[1] - HALO
    tmp[0 : n + 6] = ref[at, 0 : n + 6] + ref[at, 1 : n + 7] + ref[at, 2 : n + 8]
    return tmp[0:n] + tmp[3 : n + 3] + tmp[6 : n + 6]


def count(place, limit):
    lower = jnp.maximum(place - RADIUS, 0)
    upper = jnp.minimum(place + RADIUS, limit - 1)
    return jnp.maximum(upper - lower + 1, 1).astype(jnp.float32)


def loop(total, step, body):
    def go(i, carry):
        body(i * step)
        return carry

    lax.fori_loop(0, total // step, go, 0)


def halves_matrix():
    shape = (LANES, LANES)
    row = lax.broadcasted_iota(jnp.int32, shape, 0)
    return jnp.where((row < HALF) == (lane_ids(shape) < HALF), 1.0, 0.0).astype(jnp.bfloat16)


def frame_sum(x, ones):
    total = None
    for _ in range(3):
        part = x.astype(jnp.bfloat16)
        x = x - part.astype(jnp.float32)
        term = jnp.dot(part, ones, preferred_element_type=jnp.float32)
        total = term if total is None else total + term
    return total


def row_halo(ref, rows):
    width = ref.shape[1]
    lane = lane_ids((width, LANES))
    for k in range(HALO):
        ref[k] = jnp.where(lane >= HALF, roll(ref[rows + k], HALF), 0.0)
        ref[HALO + rows + k] = jnp.where(lane < HALF, roll(ref[HALO + k], HALF), 0.0)


def pack_kernel(rows, x_ref, out_ref, tmp):
    half = rows // 2
    low = lane_ids((GROUP, LANES)) < HALF
    for k in range(x_ref.shape[1] // LANES):
        here = slice(k * LANES, (k + 1) * LANES)
        for f in range(GROUP):
            tmp[k, f * (rows + 1) : f * (rows + 1) + rows] = x_ref[f * rows : (f + 1) * rows, here]
        for i in range(half):
            a = tmp[k, pl.ds(i, GROUP, stride=rows + 1), :]
            b = tmp[k, pl.ds(i + half, GROUP, stride=rows + 1), :]
            out_ref[2 * k, i] = jnp.where(low, a, roll(b, HALF))
            out_ref[2 * k + 1, i] = jnp.where(low, roll(a, HALF), b)


def unpack_kernel(rows, r_ref, s_ref, left_ref, right_ref):
    groups, n_row, half = r_ref.shape[0:3]
    for r in range(n_row // 2):

        def go(i):
            parts = [r_ref[g, r + h * (n_row // 2), i] for h in range(2) for g in range(groups)]
            v = jnp.transpose(jnp.concatenate(parts, axis=0))
            for k in range(2):
                at = r * rows + k * half + i
                s_ref[at] = v[k * HALF : (k + 1) * HALF]
                left_ref[at] = v[k * HALF : k * HALF + HALO]
                right_ref[at] = v[(k + 1) * HALF - HALO : (k + 1) * HALF]

        loop(half, 1, go)


def prepare(width, strip, s_ref, before_ref, after_ref, full_ref, mean_ref, area_ref, est, boxed, tmp):
    rows, cols = s_ref.shape[0:2]
    wide = cols + HALO
    height = 2 * rows
    first_col = strip() * cols - RADIUS
    ones = halves_matrix()

    def place(q0):
        for q in (q0, q0 + 1, q0 + 2, q0 + 3):
            full_ref[q + HALO, 0:HALO] = before_ref[q]
            full_ref[q + HALO, HALO : HALO + cols] = s_ref[q]
            full_ref[q + HALO, HALO + cols :] = after_ref[q]

    loop(rows, 4, place)
    row_halo(full_ref, rows)

    def first(q):
        v = full_ref[pl.ds(q, 4)]
        est[pl.ds(q, 4)] = (frame_sum(v.reshape(-1, LANES), ones) / HALF).reshape(v.shape)

    loop(rows + 2 * HALO, 4, first)

    step = rows // 8 * 3

    def down(q):
        for j in range(0, cols + 2 * HALO, 8):
            boxed[pl.ds(q, step), j : j + 8] = row_box(full_ref[pl.ds(q, step + HALO), j : j + 8])

    loop(rows + HALO, step, down)

    col = first_col + lax.broadcasted_iota(jnp.int32, (wide, LANES), 0)
    upper = jnp.where(lane_ids((8, LANES)) < HALF, 0, rows)
    col_inverse = jnp.where(
        jnp.logical_and(col >= 0, col < width), 1.0 / count(col, width), 0.0
    )

    def means(q0):
        for k in range(4):
            q = q0 + k
            row = q - RADIUS + upper
            inside = jnp.logical_and(row >= 0, row < height)
            row_inverse = jnp.where(inside, 1.0 / count(row, height), 0.0)
            area = col_inverse * jnp.concatenate([row_inverse] * (wide // 8), axis=0)
            area_ref[q] = area
            mean_ref[q] = col_box(boxed, q, tmp.at[k]) * area

    loop(rows + HALO, 4, means)


def round_kernel(first, last, width, strip, n_frame, n_row, *refs):
    if first:
        centre_ref, before_ref, after_ref = refs[0:3]
        outs, (s_ref, mean_ref, area_ref), scratch = refs[3:6], refs[6:9], refs[9:]
    else:
        e_ref, before_ref, after_ref, s_ref, mean_ref, area_ref = refs[0:6]
        outs, scratch = (refs[6:7], refs[7:]) if last else (refs[6:9], refs[9:])
    est, b1, b2, b3, slope, offset, tmp, w_buf, t_buf, flat = scratch
    rows = mean_ref.shape[0] - HALO
    cols = mean_ref.shape[1] - HALO
    ones = halves_matrix()
    edge_row = lane_ids((HALO, LANES)) % HALF

    if first:
        prepare(
            width, strip, centre_ref, before_ref, after_ref, s_ref, mean_ref, area_ref, est, b1, tmp
        )
    else:
        def place(q0):
            edges = [
                jnp.where(edge_row == q0 + k, ref[...], 0.0)
                for ref in (before_ref, after_ref)
                for k in range(8)
            ]
            v = frame_sum(jnp.concatenate(edges, axis=0), ones)
            for k in range(8):
                q = q0 + k
                est[q + HALO, 0:HALO] = v[HALO * k : HALO * (k + 1)]
                est[q + HALO, HALO : HALO + cols] = e_ref[q]
                est[q + HALO, HALO + cols :] = v[HALO * (8 + k) : HALO * (9 + k)]

        loop(rows, 8, place)
        row_halo(est, rows)

    step = rows // 8 * 3

    def down(q):
        for j in range(0, cols + 2 * HALO, 8):
            e = est[pl.ds(q, step + HALO), j : j + 8]
            b1[pl.ds(q, step), j : j + 8] = row_box(e * s_ref[pl.ds(q, step + HALO), j : j + 8])
            b2[pl.ds(q, step), j : j + 8] = row_box(e)
            b3[pl.ds(q, step), j : j + 8] = row_box(e * e)

    loop(rows + HALO, step, down)

    def fit(q0):
        for k in range(4):
            q = q0 + k
            area, mean = area_ref[q], mean_ref[q]
            guide = col_box(b2, q, tmp.at[3 * k]) * area
            variance = col_box(b3, q, tmp.at[3 * k + 1]) * area - guide * guide
            cross = col_box(b1, q, tmp.at[3 * k + 2]) * area
            a = (cross - guide * mean) / (variance + GUIDE_EPS)
            slope[q] = a
            offset[q] = mean - a * guide

    loop(rows + HALO, 4, fit)

    block = rows // 4

    def down_again(q):
        for j in range(0, cols + HALO, 8):
            b1[pl.ds(q, block), j : j + 8] = row_box(slope[pl.ds(q, block + HALO), j : j + 8])
            b2[pl.ds(q, block), j : j + 8] = row_box(offset[pl.ds(q, block + HALO), j : j + 8])

    loop(rows, block, down_again)

    lane = edge_row[0:1]

    def weigh(q0):
        for k in range(4):
            q = q0 + k
            area = area_ref[q + RADIUS, RADIUS : RADIUS + cols]
            e = est[q + HALO, HALO : HALO + cols]
            p = s_ref[q + HALO, HALO : HALO + cols]
            a = col_box(b1.at[:, 0 : cols + HALO], q, tmp.at[2 * k])
            b = col_box(b2.at[:, 0 : cols + HALO], q, tmp.at[2 * k + 1])
            gap = ((a * e + b) * area - e) * (1.0 / CAUCHY_SCALE)
            weight = 1.0 / (1.0 + gap * gap)
            w_buf[q] = weight * p
            t_buf[q] = weight

    loop(rows, 4, weigh)

    if last:
        flat[...] = jnp.zeros_like(flat)
    else:
        outs[1][...] = jnp.zeros_like(outs[1])
        outs[2][...] = jnp.zeros_like(outs[2])

    def merge(q0):
        w = frame_sum(w_buf[pl.ds(q0, 4)].reshape(4 * cols, LANES), ones)
        t = frame_sum(t_buf[pl.ds(q0, 4)].reshape(4 * cols, LANES), ones)
        new = (w / t).reshape(4, cols, LANES)
        if last:
            v = flat[...]
            for k in range(4):
                v = jnp.where(lane == q0 + k, new[k], v)
            flat[...] = v
        else:
            outs[0][pl.ds(q0, 4)] = new
            left, right = outs[1][...], outs[2][...]
            for k in range(4):
                here = edge_row == q0 + k
                left = jnp.where(here, new[k, 0:HALO], left)
                right = jnp.where(here, new[k, cols - HALO :], right)
            outs[1][...] = left
            outs[2][...] = right

    loop(rows, 4, merge)

    if last:
        shard = 2 * rows // n_row
        half = shard // 2
        turned = jnp.transpose(jnp.concatenate([flat[...], roll(flat[...], -half)], axis=0))
        for r in range(n_row):
            for f in range(n_frame):
                outs[0][f, r] = turned[r * shard : r * shard + half]


def rows_kernel(r_ref, out_ref):
    half = r_ref.shape[1]
    low = lane_ids((half, LANES)) < HALF
    for k in range(r_ref.shape[0] // 2):
        a, b = r_ref[2 * k], r_ref[2 * k + 1]
        here = slice(k * LANES, (k + 1) * LANES)
        out_ref[0:half, here] = jnp.where(low, a, roll(b, HALF))
        out_ref[half : 2 * half, here] = jnp.where(low, roll(a, HALF), b)


def strip_program(frames):
    n_frame, n_row = lax.axis_size("frame"), lax.axis_size("row")
    n_dev = n_frame * n_row
    local, rows, width = frames.shape
    half = rows // 2
    deep = rows * n_row // 2
    cols = width // n_dev
    f32 = jnp.float32

    def array(*shape):
        return jax.ShapeDtypeStruct(shape + (LANES,), f32)

    def scratch(*shape):
        return pltpu.VMEM(shape + (LANES,), f32)

    def strip():
        return lax.axis_index("frame") * n_row + lax.axis_index("row")

    packed = pl.pallas_call(
        functools.partial(pack_kernel, rows),
        grid=(4,),
        in_specs=[pl.BlockSpec((local * rows, width // 4), lambda k: (0, k))],
        out_specs=pl.BlockSpec((n_dev // 4, half, GROUP, LANES), lambda k: (k, 0, 0, 0)),
        out_shape=array(n_dev, half, GROUP),
        scratch_shapes=[scratch(width // 4 // LANES, GROUP * (rows + 1))],
        name="pack",
    )(frames.reshape(local * rows, width))

    got = lax.all_to_all(packed, BOTH, 0, 0, tiled=True)

    edge = array(deep, HALO)
    centre, left_edge, right_edge = pl.pallas_call(
        functools.partial(unpack_kernel, rows),
        out_shape=(array(deep, cols), edge, edge),
        name="unpack",
    )(got.reshape(n_frame, n_row, half, GROUP, LANES))

    up = [(i, i + 1) for i in range(n_dev - 1)]
    down = [(j, i) for i, j in up]

    def swap(to_left, to_right):
        return lax.ppermute(to_right, BOTH, up), lax.ppermute(to_left, BOTH, down)

    before, after = swap(left_edge, right_edge)
    whole = (deep + 2 * HALO, cols + 2 * HALO)
    fitted = (deep + HALO, cols + HALO)
    work = [scratch(*whole)] + [scratch(fitted[0], whole[1])] * 3 + [scratch(*fitted)] * 2
    work += [scratch(12, whole[1]), scratch(deep, cols), scratch(deep, cols), scratch(cols)]
    estimate_out = (array(deep, cols), array(HALO), array(HALO))

    def run_round(k, *operands):
        first, last = k == 0, k == ROUNDS - 1
        if last:
            out_shape = array(n_frame, n_row, half)
        elif first:
            out_shape = estimate_out + (array(*whole), array(*fitted), array(*fitted))
        else:
            out_shape = estimate_out
        return pl.pallas_call(
            functools.partial(round_kernel, first, last, width, strip, n_frame, n_row),
            out_shape=out_shape,
            scratch_shapes=work,
            name="round",
        )(*operands)

    est, left_edge, right_edge, *fixed = run_round(0, centre, before, after)
    for k in range(1, ROUNDS):
        before, after = swap(left_edge, right_edge)
        result = run_round(k, est, before, after, *fixed)
        if k < ROUNDS - 1:
            est, left_edge, right_edge = result

    got = lax.all_to_all(result.reshape(n_dev, half, LANES), BOTH, 0, 0, tiled=True)
    return pl.pallas_call(
        rows_kernel,
        out_shape=jax.ShapeDtypeStruct((rows, width), f32),
        name="rows",
    )(got)


def with_halo(x, dim, width):
    n, length = lax.axis_size("row"), x.shape[dim]
    up = [(i, i + 1) for i in range(n - 1)]
    down = [(j, i) for i, j in up]
    before = lax.ppermute(lax.slice_in_dim(x, length - width, length, axis=dim), "row", up)
    after = lax.ppermute(lax.slice_in_dim(x, 0, width, axis=dim), "row", down)
    return jnp.concatenate([before, x, after], axis=dim)


def smooth(padded_rows, area):
    length, width = padded_rows.shape[-2] - 8, padded_rows.shape[-1]
    total = sum(padded_rows[..., k : k + length, :] for k in range(9))
    padded = jnp.pad(total, [(0, 0)] * (total.ndim - 1) + [(4, 4)])
    return sum(padded[..., k : k + width] for k in range(9)) / area


def row_program(frames):
    rows, width = frames.shape[1:]
    height = rows * lax.axis_size("row")
    start = lax.axis_index("row") * rows
    total_frames = frames.shape[0] * lax.axis_size("frame")
    area = (
        count(start + jnp.arange(rows, dtype=jnp.int32), height)[:, None]
        * count(jnp.arange(width, dtype=jnp.int32), width)[None, :]
    )
    estimate = lax.psum(jnp.sum(frames, axis=0), "frame") / total_frames
    padded_frames = with_halo(frames, 1, 4)
    mean_frame = smooth(padded_frames, area)
    for _ in range(ROUNDS):
        padded = with_halo(estimate, 0, 4)
        guide = smooth(padded, area)
        variance = smooth(padded * padded, area) - guide * guide
        cross = smooth(padded[None] * padded_frames, area)
        slope = (cross - guide * mean_frame) / (variance + GUIDE_EPS)
        offset = mean_frame - slope * guide
        stacked = with_halo(jnp.stack((slope, offset)), 2, 4)
        filtered = smooth(stacked[0], area) * estimate[None] + smooth(stacked[1], area)
        gap = (filtered - estimate[None]) / CAUCHY_SCALE
        weight = 1.0 / (1.0 + gap * gap)
        sums = lax.psum((jnp.sum(weight * frames, axis=0), jnp.sum(weight, axis=0)), "frame")
        estimate = sums[0] / sums[1]
    return estimate


def shards(frames):
    local, rows, width = frames.shape
    n_dev = lax.axis_size("frame") * lax.axis_size("row")
    strips = local == GROUP and local * lax.axis_size("frame") == LANES // 2
    strips = strips and 2 * width == LANES * n_dev and rows % 16 == 0
    strips = strips and rows * lax.axis_size("row") % LANES == 0 and lax.axis_size("row") % 2 == 0
    if strips and rows * lax.axis_size("row") == LANES:
        return strip_program(frames)
    return row_program(frames)


def solution(mesh):
    return jax.shard_map(
        shards,
        mesh=mesh,
        in_specs=(P("frame", "row", None),),
        out_specs=P("row", None),
        check_vma=False,
    )
```
